512 devices in a mesh: row: 32 (over z, x_hi, core), col: 16 (over y, x_lo).
Axes of the slice: x: 4 (x_hi: 2, x_lo: 2; x = x_hi * 2 + x_lo), y: 8, z: 8, core: 2. Of those that a mesh axis runs over, the one named last changes fastest.
Arguments:
- row_desc: bfloat16 [2048, 256, 256], P(('row', 'col')), may hold values from -32 to 32, as said below
- col_desc: bfloat16 [512, 256, 256], P(('row', 'col')), may hold values from -32 to 32, as said below
- col_coords: bfloat16 [512, 2, 256], P(('row', 'col')), may hold values from -1 to 1
- row_counts: int32 [2048], replicated, may hold values from 64 to 256
- col_counts: int32 [512], replicated, may hold values from 64 to 256
- row_cluster: int32 [2048], replicated, may hold values from 0 to 7
- col_cluster: int32 [512], replicated, may hold values from 0 to 7
Outputs:
- matches: float32 [6, 2048, 3, 256], P(None, ('row', 'col'))
The draws below stay inside these ranges and needn't reach their ends.
Inputs may be any that keep to these rules, and one draw needn't show every extreme that they name: `row_desc`: custom descriptor draw. `col_desc`: custom descriptor draw.
All inputs are finite; a program needn't handle non-finite values.
Results may differ from the reference program's by a relative error of at most 0.0025.
Values may be sent and summed in bfloat16 or wider, within the bound.
No kernel may reach another device: no remote copies, remote signals or barrier semaphores. Data moves between devices by JAX's collectives and lax.ppermute only.
A program may use at most 64 MiB of HBM per device.

```python
import jax
import jax.numpy as jnp
from jax import lax

D = 256
KP = 256
RI = 4
STEPS = 6
CLUSTERS = 8
RIMG = 2048
CIMG = 512
N_ROW = 32
N_COL = 16


spread = 0.112


def paired(key):
    key_col = jax.random.fold_in(key, 11)
    key_row = jax.random.fold_in(key, 12)
    column = spread * jax.random.truncated_normal(key_col, -6.0, 6.0, (CIMG, KP, D), jnp.float32)
    rows = spread * jax.random.truncated_normal(key_row, -6.0, 6.0, (RIMG, KP, D), jnp.float32)
    return (rows, column)


def draw_row_desc(key, part):
    return paired(key)[0].astype(jnp.bfloat16)


def draw_col_desc(key, part):
    return paired(key)[1].astype(jnp.bfloat16)


def with_ends(array, stream_key, least, high):
    longest = array.shape.index(max(array.shape))
    spots = []
    for shift in (0, 1):
        where = [jax.random.randint(jax.random.fold_in(stream_key, axis), (), 0, length) for axis, length in enumerate(array.shape)]
        where[longest] = (where[longest] + shift) % array.shape[longest]
        spots.append(tuple(where))
    return array.at[spots[0]].set(least).at[spots[1]].set(high)


def shard_levels(stream_key, dims, pieces, least, top_value):
    loudness, own = 1.0, jax.random.fold_in(stream_key, 6)
    for position, shards_of in pieces:
        draws = jnp.exp(jax.random.uniform(jax.random.fold_in(own, position), (shards_of,), jnp.float32, least / len(pieces), top_value / len(pieces)))
        loudness = loudness * jnp.repeat(draws, dims[position] // shards_of).reshape([-1 if axis == position else 1 for axis in range(len(dims))])
    return loudness


def setup_inputs(seed: int = 0) -> dict:
    streams_of = jax.random.split(jax.random.key(seed), 8)
    row_desc = draw_row_desc(jax.random.fold_in(streams_of[7], 71), 0)
    col_desc = draw_col_desc(jax.random.fold_in(streams_of[7], 71), 0)
    col_coords = jnp.clip(jax.random.uniform(streams_of[2], (CIMG, 2, KP), jnp.float32, -1.0, 1.0) * shard_levels(streams_of[2], (CIMG, 2, KP), ((0, 512),), -0.4, 0.0), -1.0, 1.0).astype(jnp.bfloat16)
    row_counts = with_ends(jax.random.randint(streams_of[3], (RIMG,), max(16, KP // 4), KP + 1), jax.random.fold_in(streams_of[3], 1), max(16, KP // 4), KP).astype(jnp.int32)
    col_counts = with_ends(jax.random.randint(streams_of[4], (CIMG,), max(16, KP // 4), KP + 1), jax.random.fold_in(streams_of[4], 1), max(16, KP // 4), KP).astype(jnp.int32)
    row_cluster = with_ends(jax.random.randint(streams_of[5], (RIMG,), 0, CLUSTERS), jax.random.fold_in(streams_of[5], 1), 0, CLUSTERS - 1).astype(jnp.int32)
    col_cluster = with_ends(jax.random.randint(streams_of[6], (CIMG,), 0, CLUSTERS), jax.random.fold_in(streams_of[6], 1), 0, CLUSTERS - 1).astype(jnp.int32)
    return {"row_desc": row_desc, "col_desc": col_desc, "col_coords": col_coords, "row_counts": row_counts, "col_counts": col_counts, "row_cluster": row_cluster, "col_cluster": col_cluster}


inv_temp = 10.0
big_value = 1.0e30


def match_pair(rows, column, table, row_count, col_count):
    scores = inv_temp * jnp.dot(rows, column.T, preferred_element_type=jnp.float32)
    places = jnp.arange(rows.shape[0], dtype=jnp.int32)
    row_valid = (places < row_count)[:, None]
    col_valid = (places < col_count)[None, :]
    row_top = jnp.max(jnp.where(col_valid, scores, -big_value), axis=1, keepdims=True)
    col_top = jnp.max(jnp.where(row_valid, scores, -big_value), axis=0, keepdims=True)
    row_exp = jnp.where(col_valid, jnp.exp(jnp.where(col_valid, scores - row_top, 0.0)), 0.0)
    col_exp = jnp.where(row_valid, jnp.exp(jnp.where(row_valid, scores - col_top, 0.0)), 0.0)
    prob = (row_exp / jnp.sum(row_exp, axis=1, keepdims=True)) * (col_exp / jnp.sum(col_exp, axis=0, keepdims=True))
    prob = prob.astype(jnp.bfloat16)
    return lax.dot_general(table, prob, (((1,), (1,)), ((), ())), preferred_element_type=jnp.float32)


def reference(row_desc, col_desc, col_coords, row_counts, col_counts, row_cluster, col_cluster):
    ones = jnp.ones((col_coords.shape[0], 1, KP), jnp.bfloat16)
    tables = jnp.concatenate([ones, col_coords], axis=1)
    results = []
    for step in range(STEPS):
        def single(flat):
            block = flat // RI
            within = flat % RI
            row_pos = block // N_COL
            col_pos = block % N_COL
            image = ((row_pos * N_COL + (col_pos - step) % N_COL) * RI + within).astype(jnp.int32)
            other = (((row_pos - step) % N_ROW) * N_COL + col_pos).astype(jnp.int32)

            def working(unused):
                return match_pair(row_desc[image], col_desc[other], tables[other], row_counts[image], col_counts[other])

            def skipped(unused):
                return jnp.zeros((3, KP), jnp.float32)

            return lax.cond(row_cluster[image] == col_cluster[other], working, skipped, 0)

        results.append(lax.map(single, jnp.arange(N_ROW * N_COL * RI, dtype=jnp.int32)))
    return jnp.stack(results)
```

```python
import functools

import jax
import jax.numpy as jnp
from jax import lax
from jax.experimental import pallas as pl
from jax.experimental.pallas import tpu as pltpu
from jax.sharding import PartitionSpec as P

STEPS = 6
TABLE = 16
inv_temp = 10.0
big_value = 1e30

SMEM = pl.BlockSpec(memory_space=pltpu.SMEM)
VMEM = pl.BlockSpec(memory_space=pltpu.VMEM)


def shift(value, by_row, by_col):
    n_row, n_col = lax.axis_size("row"), lax.axis_size("col")
    perm = [
        (i * n_col + j, (i + by_row) % n_row * n_col + (j + by_col) % n_col)
        for i in range(n_row)
        for j in range(n_col)
    ]
    return lax.ppermute(value, ("row", "col"), perm)


def one_pair(rows, packed, row_count, col_count):
    k = packed.shape[0] - TABLE
    scores = inv_temp * lax.dot_general(
        packed[:k], rows, (((1,), (1,)), ((), ())), preferred_element_type=jnp.float32
    )
    col_ok = lax.broadcasted_iota(jnp.int32, scores.shape, 0) < col_count
    row_ok = lax.broadcasted_iota(jnp.int32, scores.shape, 1) < row_count
    over_col = jnp.where(col_ok, scores, -big_value)
    over_row = jnp.where(row_ok, scores, -big_value)
    row_exp = jnp.exp(over_col - jnp.max(over_col, axis=0, keepdims=True))
    col_exp = jnp.exp(over_row - jnp.max(over_row, axis=1, keepdims=True))
    row_inv = 1.0 / jnp.sum(row_exp, axis=0, keepdims=True)
    col_inv = 1.0 / jnp.sum(col_exp, axis=1, keepdims=True)
    prob = ((row_exp * row_inv) * (col_exp * col_inv)).astype(jnp.bfloat16)
    return lax.dot_general(
        packed[k:], prob, (((1,), (0,)), ((), ())), preferred_element_type=jnp.float32
    )


def panel(step, rows_ref, packed_ref, meta_ref, out_ref):
    out_ref[...] = jnp.zeros_like(out_ref)

    def body(r, carry):
        at = (step * rows_ref.shape[0] + r) * 4

        @pl.when(meta_ref[at] == 1)
        def _():
            found = one_pair(
                rows_ref[r], packed_ref[...], meta_ref[at + 1], meta_ref[at + 2]
            )
            for c in range(3):
                out_ref[c, pl.ds(r, 1), :] = found[c : c + 1]

        return carry

    lax.fori_loop(0, rows_ref.shape[0], body, 0)


def pack_kernel(col_desc, coords, packed, own, sem):
    k = col_desc.shape[1]
    copy = pltpu.make_async_copy(col_desc, packed.at[:, :k], sem)
    copy.start()
    at = lax.broadcasted_iota(jnp.int32, (TABLE, k), 0)
    x = coords[0, 0:1].astype(jnp.float32)
    y = coords[0, 1:2].astype(jnp.float32)
    zero = jnp.zeros((TABLE, k), jnp.float32)
    table = jnp.where(at == 0, 1.0, jnp.where(at == 1, x, jnp.where(at == 2, y, zero)))
    packed[0, k:] = table.astype(jnp.bfloat16)
    copy.wait()
    own[0] = packed[0]


def join_kernel(packed2, packed4, own, out):
    del own
    out[1] = packed2[0]
    out[2] = packed4[0]


def first_kernel(
    sizes, row_counts, col_counts, row_cluster, col_cluster, rows, packed, out, meta
):
    n_row, n_col = sizes
    ri = rows.shape[0]
    row_pos, col_pos = lax.axis_index("row"), lax.axis_index("col")
    for step in range(STEPS):
        odd = step % 2
        block = row_pos * n_col + lax.rem(col_pos - (step - odd) + n_col, n_col)
        image = lax.rem(row_pos - step + n_row, n_row) * n_col + lax.rem(col_pos + odd, n_col)
        for r in range(ri):
            at = (step * ri + r) * 4
            same = row_cluster[block * ri + r] == col_cluster[image]
            meta[at] = same.astype(jnp.int32)
            meta[at + 1] = row_counts[block * ri + r]
            meta[at + 2] = col_counts[image]
            meta[at + 3] = 0
    panel(0, rows, packed.at[0], meta, out)


def second_kernel(meta, rows, packed, out):
    panel(2, rows, packed.at[0], meta, out)


def odd_kernel(meta, rows0, rows2, packed, out):
    panel(1, rows0, packed.at[0], meta, out.at[0])
    panel(3, rows2, packed.at[1], meta, out.at[1])


def last_kernel(meta, rows4, packed4, packed, earlier, res0, res2, even, out):
    out[0] = earlier[0]
    out[1] = earlier[1]
    even[0] = res0[...]
    even[1] = res2[...]
    panel(5, rows4, packed.at[2], meta, out.at[2])
    panel(4, rows4, packed4.at[0], meta, even.at[2])


def final_kernel(even, home, out, sems):
    copies = []
    for n in range(3):
        copies.append(pltpu.make_async_copy(even.at[n], out.at[2 * n], sems.at[0, n]))
        copies.append(pltpu.make_async_copy(home.at[n], out.at[2 * n + 1], sems.at[1, n]))
    for copy in copies:
        copy.start()
    for copy in copies:
        copy.wait()


def near(value):
    return pltpu.with_memory_space_constraint(value, pltpu.VMEM)


def local(row_desc, col_desc, col_coords, row_counts, col_counts, row_cluster, col_cluster):
    n_row, n_col = lax.axis_size("row"), lax.axis_size("col")
    ri, slots, depth = row_desc.shape
    k = slots + TABLE

    def many(*count):
        return pltpu.VMEM((*count, 3, ri, slots), jnp.float32)

    rows2 = shift(row_desc, 0, 2)
    packed, own = pl.pallas_call(
        pack_kernel,
        out_shape=(
            pltpu.VMEM((1, k, depth), jnp.bfloat16),
            pltpu.VMEM((3, k, depth), jnp.bfloat16),
        ),
        in_specs=[pl.BlockSpec(memory_space=pl.ANY), VMEM],
        out_specs=(VMEM, VMEM),
        scratch_shapes=[pltpu.SemaphoreType.DMA(())],
        name="pack",
    )(col_desc, col_coords)
    packed4 = shift(packed, 4, 0)
    packed2 = shift(packed, 2, 0)
    rows4 = shift(rows2, 0, 2)
    joined = pl.pallas_call(
        join_kernel,
        out_shape=pltpu.VMEM((3, k, depth), jnp.bfloat16),
        in_specs=[VMEM] * 3,
        out_specs=VMEM,
        input_output_aliases={2: 0},
        name="join",
    )(near(packed2), near(packed4), near(own))
    odd = shift(joined, 1, -1)

    res0, meta = pl.pallas_call(
        functools.partial(first_kernel, (n_row, n_col)),
        out_shape=(many(), jax.ShapeDtypeStruct((STEPS * ri * 4,), jnp.int32)),
        in_specs=[SMEM] * 4 + [VMEM] * 2,
        out_specs=(VMEM, SMEM),
        name="first",
    )(row_counts, col_counts, row_cluster, col_cluster, row_desc, near(packed))
    res2 = pl.pallas_call(
        second_kernel,
        out_shape=many(),
        in_specs=[SMEM] + [VMEM] * 2,
        out_specs=VMEM,
        name="second",
    )(meta, near(rows2), near(packed2))
    res13 = pl.pallas_call(
        odd_kernel,
        out_shape=many(2),
        in_specs=[SMEM] + [VMEM] * 3,
        out_specs=VMEM,
        name="odd",
    )(meta, row_desc, near(rows2), near(odd))
    even, res135 = pl.pallas_call(
        last_kernel,
        out_shape=(many(3), many(3)),
        in_specs=[SMEM] + [VMEM] * 6,
        out_specs=(VMEM, VMEM),
        name="last",
    )(meta, near(rows4), near(packed4), near(odd), near(res13), near(res0), near(res2))
    home = shift(res135, 0, 1)
    done = pl.pallas_call(
        final_kernel,
        out_shape=jax.ShapeDtypeStruct((STEPS, 3, ri, slots), jnp.float32),
        in_specs=[VMEM] * 2,
        out_specs=pl.BlockSpec(memory_space=pl.ANY),
        scratch_shapes=[pltpu.SemaphoreType.DMA((2, 3))],
        name="final",
    )(near(even), near(home))
    return jnp.transpose(done, (0, 2, 1, 3))


def solution(mesh):
    return jax.shard_map(
        local,
        mesh=mesh,
        in_specs=(
            P(("row", "col"), None, None),
            P(("row", "col"), None, None),
            P(("row", "col"), None, None),
            P(),
            P(),
            P(),
            P(),
        ),
        out_specs=P(None, ("row", "col"), None, None),
        check_vma=False,
    )
```

```python
import functools

import jax
import jax.numpy as jnp
from jax import lax
from jax.experimental import pallas as pl
from jax.experimental.pallas import tpu as pltpu
from jax.sharding import PartitionSpec as P


STEPS = 6
TABLE = 16
inv_temp = 10.0
big_value = 1e30

SMEM = pl.BlockSpec(memory_space=pltpu.SMEM)
VMEM = pl.BlockSpec(memory_space=pltpu.VMEM)


def shift(value, by_row, by_col):
    n_row, n_col = lax.axis_size("row"), lax.axis_size("col")
    perm = [
        (i * n_col + j, (i + by_row) % n_row * n_col + (j + by_col) % n_col)
        for i in range(n_row)
        for j in range(n_col)
    ]
    return lax.ppermute(value, ("row", "col"), perm)


def one_pair(rows, packed, row_count, col_count):
    k = packed.shape[0] - TABLE
    scores = inv_temp * lax.dot_general(
        packed[:k], rows, (((1,), (1,)), ((), ())), preferred_element_type=jnp.float32
    )
    col_ok = lax.broadcasted_iota(jnp.int32, scores.shape, 0) < col_count
    row_ok = lax.broadcasted_iota(jnp.int32, scores.shape, 1) < row_count
    over_col = jnp.where(col_ok, scores, -big_value)
    over_row = jnp.where(row_ok, scores, -big_value)
    row_exp = jnp.exp(over_col - jnp.max(over_col, axis=0, keepdims=True))
    col_exp = jnp.exp(over_row - jnp.max(over_row, axis=1, keepdims=True))
    row_inv = 1.0 / jnp.sum(row_exp, axis=0, keepdims=True)
    col_inv = 1.0 / jnp.sum(col_exp, axis=1, keepdims=True)
    prob = ((row_exp * row_inv) * (col_exp * col_inv)).astype(jnp.bfloat16)
    return lax.dot_general(
        packed[k:], prob, (((1,), (0,)), ((), ())), preferred_element_type=jnp.float32
    )


def panel(step, rows_ref, packed_ref, meta_ref, out_ref):
    out_ref[...] = jnp.zeros_like(out_ref)

    def body(r, carry):
        at = (step * rows_ref.shape[0] + r) * 4

        @pl.when(meta_ref[at] == 1)
        def _():
            found = one_pair(
                rows_ref[r], packed_ref[...], meta_ref[at + 1], meta_ref[at + 2]
            )
            for c in range(3):
                out_ref[c, pl.ds(r, 1), :] = found[c : c + 1]

        return carry

    lax.fori_loop(0, rows_ref.shape[0], body, 0)


def pack_kernel(col_desc, coords, packed, table_in, sems):
    k = col_desc.shape[1]
    copies = [
        pltpu.make_async_copy(coords, table_in, sems.at[0]),
        pltpu.make_async_copy(col_desc, packed.at[:, :k], sems.at[1]),
    ]
    for copy in copies:
        copy.start()
    copies[0].wait()
    at = lax.broadcasted_iota(jnp.int32, (TABLE, k), 0)
    x = table_in[0, 0:1].astype(jnp.float32)
    y = table_in[0, 1:2].astype(jnp.float32)
    zero = jnp.zeros((TABLE, k), jnp.float32)
    table = jnp.where(at == 0, 1.0, jnp.where(at == 1, x, jnp.where(at == 2, y, zero)))
    table = table.astype(jnp.bfloat16)
    packed[0, k:] = table
    copies[1].wait()


def join_kernel(image2, image4, out):
    out[0] = image2[0]
    out[1] = image4[0]


def first_kernel(
    sizes, row_counts, col_counts, row_cluster, col_cluster, rows, packed, out, meta
):
    n_row, n_col = sizes
    ri = rows.shape[0]
    row_pos, col_pos = lax.axis_index("row"), lax.axis_index("col")
    for step in range(STEPS):
        odd = step % 2
        block = row_pos * n_col + lax.rem(col_pos - (step - odd) + n_col, n_col)
        image = lax.rem(row_pos - step + n_row, n_row) * n_col + lax.rem(col_pos + odd, n_col)
        for r in range(ri):
            at = (step * ri + r) * 4
            same = row_cluster[block * ri + r] == col_cluster[image]
            meta[at] = same.astype(jnp.int32)
            meta[at + 1] = row_counts[block * ri + r]
            meta[at + 2] = col_counts[image]
            meta[at + 3] = 0
    panel(0, rows, packed.at[0], meta, out)


def second_kernel(meta, rows, packed, out):
    panel(2, rows, packed.at[0], meta, out)


def odd_kernel(meta, rows0, rows2, rows4, image1, images, out):
    panel(1, rows0, image1.at[0], meta, out.at[0])
    panel(3, rows2, images.at[0], meta, out.at[1])
    panel(5, rows4, images.at[1], meta, out.at[2])


def fourth_kernel(meta, rows, packed, out):
    panel(4, rows, packed.at[0], meta, out)


def final_kernel(res0, res2, res4, home, out, sems):
    copies = [
        pltpu.make_async_copy(home.at[n], out.at[2 * n + 1], sems.at[n]) for n in range(3)
    ] + [
        pltpu.make_async_copy(res, out.at[2 * n], sems.at[3 + n])
        for n, res in enumerate((res0, res2, res4))
    ]
    for copy in copies:
        copy.start()
    for copy in copies:
        copy.wait()


def near(value):
    return pltpu.with_memory_space_constraint(value, pltpu.VMEM)


def local(row_desc, col_desc, col_coords, row_counts, col_counts, row_cluster, col_cluster):
    n_row, n_col = lax.axis_size("row"), lax.axis_size("col")
    ri, slots, depth = row_desc.shape
    k = slots + TABLE

    def many(*count):
        return pltpu.VMEM((*count, 3, ri, slots), jnp.float32)

    rows2 = shift(row_desc, 0, 2)
    packed = pl.pallas_call(
        pack_kernel,
        out_shape=pltpu.VMEM((1, k, depth), jnp.bfloat16),
        in_specs=[pl.BlockSpec(memory_space=pl.ANY)] * 2,
        out_specs=VMEM,
        scratch_shapes=[
            pltpu.VMEM(col_coords.shape, jnp.bfloat16),
            pltpu.SemaphoreType.DMA((2,)),
        ],
        name="pack",
    )(col_desc, col_coords)
    image2 = shift(packed, 2, 0)
    image4 = shift(packed, 4, 0)
    rows4 = shift(rows2, 0, 2)
    joined = pl.pallas_call(
        join_kernel,
        out_shape=pltpu.VMEM((2, k, depth), jnp.bfloat16),
        in_specs=[VMEM] * 2,
        out_specs=VMEM,
        name="join",
    )(near(image2), near(image4))
    images35 = shift(joined, 1, -1)
    image1 = shift(packed, 1, -1)
    rows0 = near(row_desc)

    res0, meta = pl.pallas_call(
        functools.partial(first_kernel, (n_row, n_col)),
        out_shape=(many(), jax.ShapeDtypeStruct((STEPS * ri * 4,), jnp.int32)),
        in_specs=[SMEM] * 4 + [VMEM] * 2,
        out_specs=(VMEM, SMEM),
        name="first",
    )(row_counts, col_counts, row_cluster, col_cluster, rows0, near(packed))
    res2 = pl.pallas_call(
        second_kernel,
        out_shape=many(),
        in_specs=[SMEM] + [VMEM] * 2,
        out_specs=VMEM,
        name="second",
    )(meta, near(rows2), near(image2))
    res135 = pl.pallas_call(
        odd_kernel,
        out_shape=many(3),
        in_specs=[SMEM] + [VMEM] * 5,
        out_specs=VMEM,
        name="odd",
    )(meta, rows0, near(rows2), near(rows4), near(image1), near(images35))
    home = shift(res135, 0, 1)
    res4 = pl.pallas_call(
        fourth_kernel,
        out_shape=many(),
        in_specs=[SMEM] + [VMEM] * 2,
        out_specs=VMEM,
        name="fourth",
    )(meta, near(rows4), near(image4))
    done = pl.pallas_call(
        final_kernel,
        out_shape=jax.ShapeDtypeStruct((STEPS, 3, ri, slots), jnp.float32),
        in_specs=[VMEM] * 4,
        out_specs=pl.BlockSpec(memory_space=pl.ANY),
        scratch_shapes=[pltpu.SemaphoreType.DMA((6,))],
        name="final",
    )(near(res0), near(res2), near(res4), near(home))
    return jnp.transpose(done, (0, 2, 1, 3))


def solution(mesh):
    return jax.shard_map(
        local,
        mesh=mesh,
        in_specs=(
            P(("row", "col"), None, None),
            P(("row", "col"), None, None),
            P(("row", "col"), None, None),
            P(),
            P(),
            P(),
            P(),
        ),
        out_specs=P(None, ("row", "col"), None, None),
        check_vma=False,
    )
```

```python
import functools

import jax
import jax.numpy as jnp
from jax import lax
from jax.experimental import pallas as pl
from jax.experimental.pallas import tpu as pltpu
from jax.sharding import PartitionSpec as P


STEPS = 6
TABLE = 16
COLS = 24
FLAGS = 32
inv_temp = 10.0
big_value = 1e30

SMEM = pl.BlockSpec(memory_space=pltpu.SMEM)
VMEM = pl.BlockSpec(memory_space=pltpu.VMEM)


def move(value, target, by_col):
    n_row, n_col = lax.axis_size("row"), lax.axis_size("col")
    perm = [
        (i * n_col + j, target(i) % n_row * n_col + (j + by_col) % n_col)
        for i in range(n_row)
        for j in range(n_col)
    ]
    return lax.ppermute(value, ("row", "col"), perm)


def shift(value, by_row, by_col):
    return move(value, lambda i: i + by_row, by_col)


def one_pair(rows, packed, row_count, col_count):
    k = packed.shape[0] - TABLE
    scores = inv_temp * lax.dot_general(
        packed[:k], rows, (((1,), (1,)), ((), ())), preferred_element_type=jnp.float32
    )
    col_ok = lax.broadcasted_iota(jnp.int32, scores.shape, 0) < col_count
    row_ok = lax.broadcasted_iota(jnp.int32, (1, scores.shape[1]), 1) < row_count
    over_col = jnp.where(col_ok, scores, -big_value)
    over_row = jnp.where(row_ok, scores, -big_value)
    row_exp = jnp.exp(over_col - jnp.max(over_col, axis=0, keepdims=True))
    col_exp = jnp.exp(over_row - jnp.max(over_row, axis=1, keepdims=True))
    row_inv = 1.0 / jnp.sum(row_exp, axis=0, keepdims=True)
    col_inv = 1.0 / jnp.sum(col_exp, axis=1, keepdims=True)
    prob = ((row_exp * row_inv) * (col_exp * col_inv)).astype(jnp.bfloat16)
    return lax.dot_general(
        packed[k:], prob, (((1,), (0,)), ((), ())), preferred_element_type=jnp.float32
    )


def panel(step, rows_ref, packed_ref, meta_ref, out_ref):
    ri = rows_ref.shape[0]
    out_ref[...] = jnp.zeros_like(out_ref)
    flags = jnp.max(meta_ref[pl.ds(FLAGS + step, 1), :].astype(jnp.float32)).astype(jnp.int32)

    def body(r, carry):
        @pl.when(((flags >> r) & 1) == 1)
        def _():
            found = one_pair(
                rows_ref[r],
                packed_ref[...],
                meta_ref[pl.ds(step * ri + r, 1), :],
                meta_ref[pl.ds(COLS + step, 1), :],
            )
            for c in range(3):
                out_ref[c, pl.ds(r, 1), :] = found[c : c + 1]

        return carry

    @pl.when(flags != 0)
    def _():
        lax.fori_loop(0, ri, body, 0)


def pack_kernel(col_desc, coords, packed, table_in, sems):
    k = col_desc.shape[1]
    copies = [
        pltpu.make_async_copy(coords, table_in, sems.at[0]),
        pltpu.make_async_copy(col_desc, packed.at[:, :k], sems.at[1]),
    ]
    for copy in copies:
        copy.start()
    copies[0].wait()
    at = lax.broadcasted_iota(jnp.int32, (TABLE, k), 0)
    x = table_in[0, 0:1].astype(jnp.float32)
    y = table_in[0, 1:2].astype(jnp.float32)
    zero = jnp.zeros((TABLE, k), jnp.float32)
    table = jnp.where(at == 0, 1.0, jnp.where(at == 1, x, jnp.where(at == 2, y, zero)))
    table = table.astype(jnp.bfloat16)
    packed[0, k:] = table
    copies[1].wait()


def join_kernel(image2, image4, out):
    out[0] = image2[0]
    out[1] = image4[0]


def first_kernel(
    sizes, row_counts, col_counts, row_cluster, col_cluster, rows, packed, out, meta
):
    n_row, n_col = sizes
    ri = rows.shape[0]
    row_pos, col_pos = lax.axis_index("row"), lax.axis_index("col")
    slots = rows.shape[1]
    for step in range(STEPS):
        odd = step % 2
        block = row_pos * n_col + lax.rem(col_pos - (step - odd) + n_col, n_col)
        image = lax.rem(row_pos - step + n_row, n_row) * n_col + lax.rem(col_pos + odd, n_col)
        flags = 0
        for r in range(ri):
            same = row_cluster[block * ri + r] == col_cluster[image]
            flags += same.astype(jnp.int32) * (1 << r)
            meta[pl.ds(step * ri + r, 1), :] = jnp.full(
                (1, slots), row_counts[block * ri + r], jnp.int32
            )
        meta[pl.ds(COLS + step, 1), :] = jnp.full((1, slots), col_counts[image], jnp.int32)
        meta[pl.ds(FLAGS + step, 1), :] = jnp.full((1, slots), flags, jnp.int32)
    panel(0, rows, packed.at[0], meta, out)


def second_kernel(meta, rows, packed, out):
    panel(2, rows, packed.at[0], meta, out)


def odd_kernel(meta, rows0, rows2, rows4, direct, images, out):
    even_row = lax.rem(lax.axis_index("row"), 2) == 0

    @pl.when(even_row)
    def _():
        panel(1, rows0, images.at[0], meta, out.at[0])
        panel(3, rows2, images.at[1], meta, out.at[1])
        panel(5, rows4, direct.at[0], meta, out.at[2])

    @pl.when(jnp.logical_not(even_row))
    def _():
        panel(1, rows0, direct.at[0], meta, out.at[0])
        panel(3, rows2, images.at[0], meta, out.at[1])
        panel(5, rows4, images.at[1], meta, out.at[2])


def fourth_kernel(meta, rows, packed, out):
    panel(4, rows, packed.at[0], meta, out)


def final_kernel(res0, res2, res4, home, out, sems):
    copies = [
        pltpu.make_async_copy(home.at[n], out.at[2 * n + 1], sems.at[n]) for n in range(3)
    ] + [
        pltpu.make_async_copy(res, out.at[2 * n], sems.at[3 + n])
        for n, res in enumerate((res0, res2, res4))
    ]
    for copy in copies:
        copy.start()
    for copy in copies:
        copy.wait()


def near(value):
    return pltpu.with_memory_space_constraint(value, pltpu.VMEM)


def local(row_desc, col_desc, col_coords, row_counts, col_counts, row_cluster, col_cluster):
    n_row, n_col = lax.axis_size("row"), lax.axis_size("col")
    ri, slots, depth = row_desc.shape
    k = slots + TABLE

    def many(*count):
        return pltpu.VMEM((*count, 3, ri, slots), jnp.float32)

    rows2 = shift(row_desc, 0, 2)
    packed = pl.pallas_call(
        pack_kernel,
        out_shape=pltpu.VMEM((1, k, depth), jnp.bfloat16),
        in_specs=[pl.BlockSpec(memory_space=pl.ANY)] * 2,
        out_specs=VMEM,
        scratch_shapes=[
            pltpu.VMEM(col_coords.shape, jnp.bfloat16),
            pltpu.SemaphoreType.DMA((2,)),
        ],
        name="pack",
    )(col_desc, col_coords)
    image2 = shift(packed, 2, 0)
    image4 = shift(packed, 4, 0)
    rows4 = shift(rows2, 0, 2)
    joined = pl.pallas_call(
        join_kernel,
        out_shape=pltpu.VMEM((2, k, depth), jnp.bfloat16),
        in_specs=[VMEM] * 2,
        out_specs=VMEM,
        name="join",
    )(near(image2), near(image4))
    images = move(joined, lambda i: i ^ 1, -1)
    direct = move(packed, lambda i: i + (5 if i % 2 else 1), -1)
    rows0 = near(row_desc)

    res0, meta = pl.pallas_call(
        functools.partial(first_kernel, (n_row, n_col)),
        out_shape=(many(), pltpu.VMEM((FLAGS + 8, slots), jnp.int32)),
        in_specs=[SMEM] * 4 + [VMEM] * 2,
        out_specs=(VMEM, VMEM),
        name="first",
    )(row_counts, col_counts, row_cluster, col_cluster, rows0, near(packed))
    res2 = pl.pallas_call(
        second_kernel,
        out_shape=many(),
        in_specs=[VMEM] * 3,
        out_specs=VMEM,
        name="second",
    )(near(meta), near(rows2), near(image2))
    res135 = pl.pallas_call(
        odd_kernel,
        out_shape=many(3),
        in_specs=[VMEM] * 6,
        out_specs=VMEM,
        name="odd",
    )(near(meta), rows0, near(rows2), near(rows4), near(direct), near(images))
    home = shift(res135, 0, 1)
    res4 = pl.pallas_call(
        fourth_kernel,
        out_shape=many(),
        in_specs=[VMEM] * 3,
        out_specs=VMEM,
        name="fourth",
    )(near(meta), near(rows4), near(image4))
    done = pl.pallas_call(
        final_kernel,
        out_shape=jax.ShapeDtypeStruct((STEPS, 3, ri, slots), jnp.float32),
        in_specs=[VMEM] * 4,
        out_specs=pl.BlockSpec(memory_space=pl.ANY),
        scratch_shapes=[pltpu.SemaphoreType.DMA((6,))],
        name="final",
    )(near(res0), near(res2), near(res4), near(home))
    return jnp.transpose(done, (0, 2, 1, 3))


def solution(mesh):
    return jax.shard_map(
        local,
        mesh=mesh,
        in_specs=(
            P(("row", "col"), None, None),
            P(("row", "col"), None, None),
            P(("row", "col"), None, None),
            P(),
            P(),
            P(),
            P(),
        ),
        out_specs=P(None, ("row", "col"), None, None),
        check_vma=False,
    )
```

```python
import functools

import jax
import jax.numpy as jnp
from jax import lax
from jax.experimental import pallas as pl
from jax.experimental.pallas import tpu as pltpu
from jax.sharding import PartitionSpec as P


STEPS = 6
TABLE = 16
COLS = 24
FLAGS = 32
inv_temp = 10.0
big_value = 1e30

SMEM = pl.BlockSpec(memory_space=pltpu.SMEM)
VMEM = pl.BlockSpec(memory_space=pltpu.VMEM)


def move(value, target, by_col):
    n_row, n_col = lax.axis_size("row"), lax.axis_size("col")
    perm = [
        (i * n_col + j, target(i) % n_row * n_col + (j + by_col) % n_col)
        for i in range(n_row)
        for j in range(n_col)
    ]
    return lax.ppermute(value, ("row", "col"), perm)


def shift(value, by_row, by_col):
    return move(value, lambda i: i + by_row, by_col)


def one_pair(rows, packed, row_count, col_count):
    k = packed.shape[0] - TABLE
    scores = inv_temp * lax.dot_general(
        packed[:k], rows, (((1,), (1,)), ((), ())), preferred_element_type=jnp.float32
    )
    col_ok = lax.broadcasted_iota(jnp.int32, scores.shape, 0) < col_count
    row_ok = lax.broadcasted_iota(jnp.int32, (1, scores.shape[1]), 1) < row_count
    over_col = jnp.where(col_ok, scores, -big_value)
    over_row = jnp.where(row_ok, scores, -big_value)
    row_exp = jnp.exp(over_col - jnp.max(over_col, axis=0, keepdims=True))
    col_exp = jnp.exp(over_row - jnp.max(over_row, axis=1, keepdims=True))
    row_inv = 1.0 / jnp.sum(row_exp, axis=0, keepdims=True)
    col_inv = 1.0 / jnp.sum(col_exp, axis=1, keepdims=True)
    prob = ((row_exp * row_inv) * (col_exp * col_inv)).astype(jnp.bfloat16)
    return lax.dot_general(
        packed[k:], prob, (((1,), (0,)), ((), ())), preferred_element_type=jnp.float32
    )


def panel(step, rows_ref, packed_ref, meta_ref, out_ref):
    ri = rows_ref.shape[0]
    out_ref[...] = jnp.zeros_like(out_ref)
    flags = jnp.max(meta_ref[pl.ds(FLAGS + step, 1), :].astype(jnp.float32)).astype(jnp.int32)

    def body(r, carry):
        @pl.when(((flags >> r) & 1) == 1)
        def _():
            found = one_pair(
                rows_ref[r],
                packed_ref[...],
                meta_ref[pl.ds(step * ri + r, 1), :],
                meta_ref[pl.ds(COLS + step, 1), :],
            )
            for c in range(3):
                out_ref[c, pl.ds(r, 1), :] = found[c : c + 1]

        return carry

    @pl.when(flags != 0)
    def _():
        lax.fori_loop(0, ri, body, 0)


def pack_kernel(col_desc, coords, packed, table_in, sems):
    k = col_desc.shape[1]
    copies = [
        pltpu.make_async_copy(coords, table_in, sems.at[0]),
        pltpu.make_async_copy(col_desc, packed.at[:, :k], sems.at[1]),
    ]
    for copy in copies:
        copy.start()
    copies[0].wait()
    at = lax.broadcasted_iota(jnp.int32, (TABLE, k), 0)
    x = table_in[0, 0:1].astype(jnp.float32)
    y = table_in[0, 1:2].astype(jnp.float32)
    zero = jnp.zeros((TABLE, k), jnp.float32)
    table = jnp.where(at == 0, 1.0, jnp.where(at == 1, x, jnp.where(at == 2, y, zero)))
    table = table.astype(jnp.bfloat16)
    packed[0, k:] = table
    copies[1].wait()


def join_kernel(image2, image4, out):
    out[0] = image2[0]
    out[1] = image4[0]


def first_kernel(
    sizes, row_counts, col_counts, row_cluster, col_cluster, rows, packed, out, meta
):
    n_row, n_col = sizes
    ri = rows.shape[0]
    row_pos, col_pos = lax.axis_index("row"), lax.axis_index("col")
    slots = rows.shape[1]
    for step in range(STEPS):
        odd = step % 2
        block = row_pos * n_col + lax.rem(col_pos - (step - odd) + n_col, n_col)
        image = lax.rem(row_pos - step + n_row, n_row) * n_col + lax.rem(col_pos + odd, n_col)
        flags = 0
        for r in range(ri):
            same = row_cluster[block * ri + r] == col_cluster[image]
            flags += same.astype(jnp.int32) * (1 << r)
            meta[pl.ds(step * ri + r, 1), :] = jnp.full(
                (1, slots), row_counts[block * ri + r], jnp.int32
            )
        meta[pl.ds(COLS + step, 1), :] = jnp.full((1, slots), col_counts[image], jnp.int32)
        meta[pl.ds(FLAGS + step, 1), :] = jnp.full((1, slots), flags, jnp.int32)
    panel(0, rows, packed.at[0], meta, out)


def even_row():
    return lax.rem(lax.axis_index("row"), 2) == 0


def early_kernel(meta, rows0, rows2, image2, direct, res2, out):
    panel(2, rows2, image2.at[0], meta, res2)

    @pl.when(jnp.logical_not(even_row()))
    def _():
        panel(1, rows0, direct.at[0], meta, out.at[0])


def middle_kernel(meta, rows0, rows2, images, kept, out):
    del kept
    even = even_row()

    @pl.when(even)
    def _():
        panel(1, rows0, images.at[0], meta, out.at[0])

    panel(3, rows2, images.at[even.astype(jnp.int32)], meta, out.at[1])


def late_kernel(meta, rows4, direct, images, kept, out):
    del kept
    even = even_row()

    @pl.when(even)
    def _():
        panel(5, rows4, direct.at[0], meta, out.at[2])

    @pl.when(jnp.logical_not(even))
    def _():
        panel(5, rows4, images.at[1], meta, out.at[2])


def fourth_kernel(meta, rows, packed, out):
    panel(4, rows, packed.at[0], meta, out)


def final_kernel(res0, res2, res4, home, out, sems):
    copies = [
        pltpu.make_async_copy(home.at[n], out.at[2 * n + 1], sems.at[n]) for n in range(3)
    ] + [
        pltpu.make_async_copy(res, out.at[2 * n], sems.at[3 + n])
        for n, res in enumerate((res0, res2, res4))
    ]
    for copy in copies:
        copy.start()
    for copy in copies:
        copy.wait()


def near(value):
    return pltpu.with_memory_space_constraint(value, pltpu.VMEM)


def local(row_desc, col_desc, col_coords, row_counts, col_counts, row_cluster, col_cluster):
    n_row, n_col = lax.axis_size("row"), lax.axis_size("col")
    ri, slots, depth = row_desc.shape
    k = slots + TABLE

    def many(*count):
        return pltpu.VMEM((*count, 3, ri, slots), jnp.float32)

    rows2 = shift(row_desc, 0, 2)
    packed = pl.pallas_call(
        pack_kernel,
        out_shape=pltpu.VMEM((1, k, depth), jnp.bfloat16),
        in_specs=[pl.BlockSpec(memory_space=pl.ANY)] * 2,
        out_specs=VMEM,
        scratch_shapes=[
            pltpu.VMEM(col_coords.shape, jnp.bfloat16),
            pltpu.SemaphoreType.DMA((2,)),
        ],
        name="pack",
    )(col_desc, col_coords)
    image2 = shift(packed, 2, 0)
    image4 = shift(packed, 4, 0)
    rows4 = shift(rows2, 0, 2)
    joined = pl.pallas_call(
        join_kernel,
        out_shape=pltpu.VMEM((2, k, depth), jnp.bfloat16),
        in_specs=[VMEM] * 2,
        out_specs=VMEM,
        name="join",
    )(near(image2), near(image4))
    images = move(joined, lambda i: i ^ 1, -1)
    direct = move(packed, lambda i: i + (5 if i % 2 else 1), -1)
    rows0 = near(row_desc)

    res0, meta = pl.pallas_call(
        functools.partial(first_kernel, (n_row, n_col)),
        out_shape=(many(), pltpu.VMEM((FLAGS + 8, slots), jnp.int32)),
        in_specs=[SMEM] * 4 + [VMEM] * 2,
        out_specs=(VMEM, VMEM),
        name="first",
    )(row_counts, col_counts, row_cluster, col_cluster, rows0, near(packed))
    meta = near(meta)
    rows2, rows4, image2 = near(rows2), near(rows4), near(image2)
    direct, images = near(direct), near(images)
    res2, res135 = pl.pallas_call(
        early_kernel,
        out_shape=(many(), many(3)),
        in_specs=[VMEM] * 5,
        out_specs=(VMEM, VMEM),
        name="early",
    )(meta, rows0, rows2, image2, direct)
    res135 = pl.pallas_call(
        middle_kernel,
        out_shape=many(3),
        in_specs=[VMEM] * 5,
        out_specs=VMEM,
        input_output_aliases={4: 0},
        name="middle",
    )(meta, rows0, rows2, images, near(res135))
    res135 = pl.pallas_call(
        late_kernel,
        out_shape=many(3),
        in_specs=[VMEM] * 5,
        out_specs=VMEM,
        input_output_aliases={4: 0},
        name="late",
    )(meta, rows4, direct, images, near(res135))
    home = shift(res135, 0, 1)
    res4 = pl.pallas_call(
        fourth_kernel,
        out_shape=many(),
        in_specs=[VMEM] * 3,
        out_specs=VMEM,
        name="fourth",
    )(meta, rows4, near(image4))
    done = pl.pallas_call(
        final_kernel,
        out_shape=jax.ShapeDtypeStruct((STEPS, 3, ri, slots), jnp.float32),
        in_specs=[VMEM] * 4,
        out_specs=pl.BlockSpec(memory_space=pl.ANY),
        scratch_shapes=[pltpu.SemaphoreType.DMA((6,))],
        name="final",
    )(near(res0), near(res2), near(res4), near(home))
    return jnp.transpose(done, (0, 2, 1, 3))


def solution(mesh):
    return jax.shard_map(
        local,
        mesh=mesh,
        in_specs=(
            P(("row", "col"), None, None),
            P(("row", "col"), None, None),
            P(("row", "col"), None, None),
            P(),
            P(),
            P(),
            P(),
        ),
        out_specs=P(None, ("row", "col"), None, None),
        check_vma=False,
    )
```

```python
import functools

import jax
import jax.numpy as jnp
from jax import lax
from jax.experimental import pallas as pl
from jax.experimental.pallas import tpu as pltpu
from jax.sharding import PartitionSpec as P


STEPS = 6
TABLE = 8
PARTS = 4
COLS = 24
FLAGS = 32
inv_temp = 10.0
big_value = 1e30

SMEM = pl.BlockSpec(memory_space=pltpu.SMEM)
VMEM = pl.BlockSpec(memory_space=pltpu.VMEM)


def move(value, target, by_col):
    n_row, n_col = lax.axis_size("row"), lax.axis_size("col")
    perm = [
        (i * n_col + j, target(i) % n_row * n_col + (j + by_col) % n_col)
        for i in range(n_row)
        for j in range(n_col)
    ]
    return lax.ppermute(value, ("row", "col"), perm)


def shift(value, by_row, by_col):
    return move(value, lambda i: i + by_row, by_col)


def one_pair(rows, packed, row_count, col_count):
    k = packed.shape[0] - TABLE
    scores = inv_temp * lax.dot_general(
        packed[:k], rows, (((1,), (1,)), ((), ())), preferred_element_type=jnp.float32
    )
    col_ok = lax.broadcasted_iota(jnp.int32, scores.shape, 0) < col_count
    row_ok = lax.broadcasted_iota(jnp.int32, (1, scores.shape[1]), 1) < row_count
    over_col = jnp.where(col_ok, scores, -big_value)
    over_row = jnp.where(row_ok, scores, -big_value)
    row_exp = jnp.exp(over_col - jnp.max(over_col, axis=0, keepdims=True))
    col_exp = jnp.exp(over_row - jnp.max(over_row, axis=1, keepdims=True))
    row_inv = 1.0 / jnp.sum(row_exp, axis=0, keepdims=True)
    col_inv = 1.0 / jnp.sum(col_exp, axis=1, keepdims=True)
    prob = ((row_exp * row_inv) * (col_exp * col_inv)).astype(jnp.bfloat16)
    return lax.dot_general(
        packed[k:], prob, (((1,), (0,)), ((), ())), preferred_element_type=jnp.float32
    )


def panel(step, rows_ref, packed_ref, meta_ref, out_ref):
    ri = rows_ref.shape[0]
    out_ref[...] = jnp.zeros_like(out_ref)
    flags = jnp.max(meta_ref[pl.ds(FLAGS + step, 1), :].astype(jnp.float32)).astype(jnp.int32)

    def body(r, carry):
        @pl.when(((flags >> r) & 1) == 1)
        def _():
            found = one_pair(
                rows_ref[r],
                packed_ref[...],
                meta_ref[pl.ds(step * ri + r, 1), :],
                meta_ref[pl.ds(COLS + step, 1), :],
            )
            for c in range(3):
                out_ref[c, pl.ds(r, 1), :] = found[c : c + 1]

        return carry

    @pl.when(flags != 0)
    def _():
        lax.fori_loop(0, ri, body, 0)


def pack_kernel(col_desc, coords, packed, table_in, sems):
    k = col_desc.shape[1]
    part = k // PARTS
    copies = [pltpu.make_async_copy(coords, table_in, sems.at[0])] + [
        pltpu.make_async_copy(
            col_desc.at[:, n * part : (n + 1) * part],
            packed.at[:, n * part : (n + 1) * part],
            sems.at[n + 1],
        )
        for n in range(PARTS)
    ]
    for copy in copies:
        copy.start()
    copies[0].wait()
    at = lax.broadcasted_iota(jnp.int32, (TABLE, k), 0)
    x = table_in[0, 0:1].astype(jnp.float32)
    y = table_in[0, 1:2].astype(jnp.float32)
    zero = jnp.zeros((TABLE, k), jnp.float32)
    table = jnp.where(at == 0, 1.0, jnp.where(at == 1, x, jnp.where(at == 2, y, zero)))
    table = table.astype(jnp.bfloat16)
    packed[0, k:] = table
    for copy in copies[1:]:
        copy.wait()


def join_kernel(image2, image4, out):
    out[0] = image2[0]
    out[1] = image4[0]


def first_kernel(
    sizes, row_counts, col_counts, row_cluster, col_cluster, rows, packed, out, meta
):
    n_row, n_col = sizes
    ri = rows.shape[0]
    row_pos, col_pos = lax.axis_index("row"), lax.axis_index("col")
    slots = rows.shape[1]
    for step in range(STEPS):
        odd = step % 2
        block = row_pos * n_col + lax.rem(col_pos - (step - odd) + n_col, n_col)
        image = lax.rem(row_pos - step + n_row, n_row) * n_col + lax.rem(col_pos + odd, n_col)
        flags = 0
        for r in range(ri):
            same = row_cluster[block * ri + r] == col_cluster[image]
            flags += same.astype(jnp.int32) * (1 << r)
            meta[pl.ds(step * ri + r, 1), :] = jnp.full(
                (1, slots), row_counts[block * ri + r], jnp.int32
            )
        meta[pl.ds(COLS + step, 1), :] = jnp.full((1, slots), col_counts[image], jnp.int32)
        meta[pl.ds(FLAGS + step, 1), :] = jnp.full((1, slots), flags, jnp.int32)
    panel(0, rows, packed.at[0], meta, out)


def even_row():
    return lax.rem(lax.axis_index("row"), 2) == 0


def early_kernel(meta, rows0, rows2, image2, direct, res2, out):
    panel(2, rows2, image2.at[0], meta, res2)

    @pl.when(jnp.logical_not(even_row()))
    def _():
        panel(1, rows0, direct.at[0], meta, out.at[0])


def middle_kernel(meta, rows0, rows2, images, kept, out):
    del kept
    even = even_row()

    @pl.when(even)
    def _():
        panel(1, rows0, images.at[0], meta, out.at[0])

    panel(3, rows2, images.at[even.astype(jnp.int32)], meta, out.at[1])


def late_kernel(meta, rows4, direct, images, kept, out):
    del kept
    even = even_row()

    @pl.when(even)
    def _():
        panel(5, rows4, direct.at[0], meta, out.at[2])

    @pl.when(jnp.logical_not(even))
    def _():
        panel(5, rows4, images.at[1], meta, out.at[2])


def fourth_kernel(meta, rows, packed, out):
    panel(4, rows, packed.at[0], meta, out)


def final_kernel(res0, res2, res4, home, out, sems):
    copies = [
        pltpu.make_async_copy(home.at[n], out.at[2 * n + 1], sems.at[n]) for n in range(3)
    ] + [
        pltpu.make_async_copy(res, out.at[2 * n], sems.at[3 + n])
        for n, res in enumerate((res0, res2, res4))
    ]
    for copy in copies:
        copy.start()
    for copy in copies:
        copy.wait()


def near(value):
    return pltpu.with_memory_space_constraint(value, pltpu.VMEM)


def local(row_desc, col_desc, col_coords, row_counts, col_counts, row_cluster, col_cluster):
    n_row, n_col = lax.axis_size("row"), lax.axis_size("col")
    ri, slots, depth = row_desc.shape
    k = slots + TABLE

    def many(*count):
        return pltpu.VMEM((*count, 3, ri, slots), jnp.float32)

    rows2 = shift(row_desc, 0, 2)
    packed = pl.pallas_call(
        pack_kernel,
        out_shape=pltpu.VMEM((1, k, depth), jnp.bfloat16),
        in_specs=[pl.BlockSpec(memory_space=pl.ANY)] * 2,
        out_specs=VMEM,
        scratch_shapes=[
            pltpu.VMEM(col_coords.shape, jnp.bfloat16),
            pltpu.SemaphoreType.DMA((PARTS + 1,)),
        ],
        name="pack",
    )(col_desc, col_coords)
    image2 = shift(packed, 2, 0)
    image4 = shift(packed, 4, 0)
    rows4 = shift(rows2, 0, 2)
    joined = pl.pallas_call(
        join_kernel,
        out_shape=pltpu.VMEM((2, k, depth), jnp.bfloat16),
        in_specs=[VMEM] * 2,
        out_specs=VMEM,
        name="join",
    )(near(image2), near(image4))
    images = move(joined, lambda i: i ^ 1, -1)
    direct = move(packed, lambda i: i + (5 if i % 2 else 1), -1)
    rows0 = near(row_desc)

    res0, meta = pl.pallas_call(
        functools.partial(first_kernel, (n_row, n_col)),
        out_shape=(many(), pltpu.VMEM((FLAGS + 8, slots), jnp.int32)),
        in_specs=[SMEM] * 4 + [VMEM] * 2,
        out_specs=(VMEM, VMEM),
        name="first",
    )(row_counts, col_counts, row_cluster, col_cluster, rows0, near(packed))
    meta = near(meta)
    rows2, rows4, image2 = near(rows2), near(rows4), near(image2)
    direct, images = near(direct), near(images)
    res2, res135 = pl.pallas_call(
        early_kernel,
        out_shape=(many(), many(3)),
        in_specs=[VMEM] * 5,
        out_specs=(VMEM, VMEM),
        name="early",
    )(meta, rows0, rows2, image2, direct)
    res135 = pl.pallas_call(
        middle_kernel,
        out_shape=many(3),
        in_specs=[VMEM] * 5,
        out_specs=VMEM,
        input_output_aliases={4: 0},
        name="middle",
    )(meta, rows0, rows2, images, near(res135))
    res135 = pl.pallas_call(
        late_kernel,
        out_shape=many(3),
        in_specs=[VMEM] * 5,
        out_specs=VMEM,
        input_output_aliases={4: 0},
        name="late",
    )(meta, rows4, direct, images, near(res135))
    home = shift(res135, 0, 1)
    res4 = pl.pallas_call(
        fourth_kernel,
        out_shape=many(),
        in_specs=[VMEM] * 3,
        out_specs=VMEM,
        name="fourth",
    )(meta, rows4, near(image4))
    done = pl.pallas_call(
        final_kernel,
        out_shape=jax.ShapeDtypeStruct((STEPS, 3, ri, slots), jnp.float32),
        in_specs=[VMEM] * 4,
        out_specs=pl.BlockSpec(memory_space=pl.ANY),
        scratch_shapes=[pltpu.SemaphoreType.DMA((6,))],
        name="final",
    )(near(res0), near(res2), near(res4), near(home))
    return jnp.transpose(done, (0, 2, 1, 3))


def solution(mesh):
    return jax.shard_map(
        local,
        mesh=mesh,
        in_specs=(
            P(("row", "col"), None, None),
            P(("row", "col"), None, None),
            P(("row", "col"), None, None),
            P(),
            P(),
            P(),
            P(),
        ),
        out_specs=P(None, ("row", "col"), None, None),
        check_vma=False,
    )
```

```python
import functools

import jax
import jax.numpy as jnp
from jax import lax
from jax.experimental import pallas as pl
from jax.experimental.pallas import tpu as pltpu
from jax.sharding import PartitionSpec as P


STEPS = 6
TABLE = 8
PARTS = 4
COLS = 24
FLAGS = 32
inv_temp = 10.0
big_value = 1e30

SMEM = pl.BlockSpec(memory_space=pltpu.SMEM)
VMEM = pl.BlockSpec(memory_space=pltpu.VMEM)


def move(value, target, by_col):
    n_row, n_col = lax.axis_size("row"), lax.axis_size("col")
    perm = [
        (i * n_col + j, target(i) % n_row * n_col + (j + by_col) % n_col)
        for i in range(n_row)
        for j in range(n_col)
    ]
    return lax.ppermute(value, ("row", "col"), perm)


def shift(value, by_row, by_col):
    return move(value, lambda i: i + by_row, by_col)


def one_pair(rows, packed, row_count, col_count):
    k = packed.shape[0] - TABLE
    scores = inv_temp * lax.dot_general(
        packed[:k], rows, (((1,), (1,)), ((), ())), preferred_element_type=jnp.float32
    )
    col_ok = lax.broadcasted_iota(jnp.int32, scores.shape, 0) < col_count
    row_ok = lax.broadcasted_iota(jnp.int32, (1, scores.shape[1]), 1) < row_count
    over_col = jnp.where(col_ok, scores, -big_value)
    over_row = jnp.where(row_ok, scores, -big_value)
    row_exp = jnp.exp(over_col - jnp.max(over_col, axis=0, keepdims=True))
    col_exp = jnp.exp(over_row - jnp.max(over_row, axis=1, keepdims=True))
    row_inv = 1.0 / jnp.sum(row_exp, axis=0, keepdims=True)
    col_inv = 1.0 / jnp.sum(col_exp, axis=1, keepdims=True)
    prob = ((row_exp * row_inv) * (col_exp * col_inv)).astype(jnp.bfloat16)
    return lax.dot_general(
        packed[k:], prob, (((1,), (0,)), ((), ())), preferred_element_type=jnp.float32
    )


def panel(step, rows_ref, packed_ref, meta_ref, out_ref):
    ri = rows_ref.shape[0]
    out_ref[...] = jnp.zeros_like(out_ref)
    flags = jnp.max(meta_ref[pl.ds(FLAGS + step, 1), :].astype(jnp.float32)).astype(jnp.int32)

    def body(r, carry):
        @pl.when(((flags >> r) & 1) == 1)
        def _():
            found = one_pair(
                rows_ref[r],
                packed_ref[...],
                meta_ref[pl.ds(step * ri + r, 1), :],
                meta_ref[pl.ds(COLS + step, 1), :],
            )
            for c in range(3):
                out_ref[c, pl.ds(r, 1), :] = found[c : c + 1]

        return carry

    @pl.when(flags != 0)
    def _():
        lax.fori_loop(0, ri, body, 0)


def pack_kernel(col_desc, coords, packed, table_in, sems):
    k = col_desc.shape[1]
    part = k // PARTS
    copies = [pltpu.make_async_copy(coords, table_in, sems.at[0])] + [
        pltpu.make_async_copy(
            col_desc.at[:, n * part : (n + 1) * part],
            packed.at[:, n * part : (n + 1) * part],
            sems.at[n + 1],
        )
        for n in range(PARTS)
    ]
    for copy in copies:
        copy.start()
    copies[0].wait()
    at = lax.broadcasted_iota(jnp.int32, (TABLE, k), 0)
    x = table_in[0, 0:1].astype(jnp.float32)
    y = table_in[0, 1:2].astype(jnp.float32)
    zero = jnp.zeros((TABLE, k), jnp.float32)
    table = jnp.where(at == 0, 1.0, jnp.where(at == 1, x, jnp.where(at == 2, y, zero)))
    table = table.astype(jnp.bfloat16)
    packed[0, k:] = table
    for copy in copies[1:]:
        copy.wait()


def join_kernel(image2, image4, out):
    out[0] = image2[0]
    out[1] = image4[0]


def first_kernel(
    sizes, row_counts, col_counts, row_cluster, col_cluster, rows, packed, out, meta
):
    n_row, n_col = sizes
    ri = rows.shape[0]
    row_pos, col_pos = lax.axis_index("row"), lax.axis_index("col")
    slots = rows.shape[1]
    for step in range(STEPS):
        odd = step % 2
        block = row_pos * n_col + lax.rem(col_pos - (step - odd) + n_col, n_col)
        image = lax.rem(row_pos - step + n_row, n_row) * n_col + lax.rem(col_pos + odd, n_col)
        flags = 0
        for r in range(ri):
            same = row_cluster[block * ri + r] == col_cluster[image]
            flags += same.astype(jnp.int32) * (1 << r)
            meta[pl.ds(step * ri + r, 1), :] = jnp.full(
                (1, slots), row_counts[block * ri + r], jnp.int32
            )
        meta[pl.ds(COLS + step, 1), :] = jnp.full((1, slots), col_counts[image], jnp.int32)
        meta[pl.ds(FLAGS + step, 1), :] = jnp.full((1, slots), flags, jnp.int32)
    panel(0, rows, packed.at[0], meta, out)


def even_row():
    return lax.rem(lax.axis_index("row"), 2) == 0


def early_kernel(meta, rows0, rows2, image2, direct, res2, out):
    panel(2, rows2, image2.at[0], meta, res2)

    @pl.when(jnp.logical_not(even_row()))
    def _():
        panel(1, rows0, direct.at[0], meta, out.at[0])


def middle_kernel(meta, rows0, rows2, images, kept, out):
    del kept
    even = even_row()

    @pl.when(even)
    def _():
        panel(1, rows0, images.at[0], meta, out.at[0])

    panel(3, rows2, images.at[even.astype(jnp.int32)], meta, out.at[1])


def late_kernel(meta, rows4, direct, images, kept, out):
    del kept
    even = even_row()

    @pl.when(even)
    def _():
        panel(5, rows4, direct.at[0], meta, out.at[2])

    @pl.when(jnp.logical_not(even))
    def _():
        panel(5, rows4, images.at[1], meta, out.at[2])


def write_all(parts, out, sems):
    copies = [
        pltpu.make_async_copy(part, out.at[at], sems.at[n])
        for n, (part, at) in enumerate(parts)
    ]
    for copy in copies:
        copy.start()
    for copy in copies:
        copy.wait()


def fourth_kernel(meta, rows, packed, res0, res2, out, res4, sems):
    panel(4, rows, packed.at[0], meta, res4)
    write_all(((res0, 0), (res2, 2), (res4, 4)), out, sems)


def final_kernel(home, kept, out, sems):
    del kept
    write_all([(home.at[n], 2 * n + 1) for n in range(3)], out, sems)


def near(value):
    return pltpu.with_memory_space_constraint(value, pltpu.VMEM)


def local(row_desc, col_desc, col_coords, row_counts, col_counts, row_cluster, col_cluster):
    n_row, n_col = lax.axis_size("row"), lax.axis_size("col")
    ri, slots, depth = row_desc.shape
    k = slots + TABLE

    def many(*count):
        return pltpu.VMEM((*count, 3, ri, slots), jnp.float32)

    rows2 = shift(row_desc, 0, 2)
    packed = pl.pallas_call(
        pack_kernel,
        out_shape=pltpu.VMEM((1, k, depth), jnp.bfloat16),
        in_specs=[pl.BlockSpec(memory_space=pl.ANY)] * 2,
        out_specs=VMEM,
        scratch_shapes=[
            pltpu.VMEM(col_coords.shape, jnp.bfloat16),
            pltpu.SemaphoreType.DMA((PARTS + 1,)),
        ],
        name="pack",
    )(col_desc, col_coords)
    image2 = shift(packed, 2, 0)
    image4 = shift(packed, 4, 0)
    rows4 = shift(rows2, 0, 2)
    joined = pl.pallas_call(
        join_kernel,
        out_shape=pltpu.VMEM((2, k, depth), jnp.bfloat16),
        in_specs=[VMEM] * 2,
        out_specs=VMEM,
        name="join",
    )(near(image2), near(image4))
    images = move(joined, lambda i: i ^ 1, -1)
    direct = move(packed, lambda i: i + (5 if i % 2 else 1), -1)
    rows0 = near(row_desc)

    res0, meta = pl.pallas_call(
        functools.partial(first_kernel, (n_row, n_col)),
        out_shape=(many(), pltpu.VMEM((FLAGS + 8, slots), jnp.int32)),
        in_specs=[SMEM] * 4 + [VMEM] * 2,
        out_specs=(VMEM, VMEM),
        name="first",
    )(row_counts, col_counts, row_cluster, col_cluster, rows0, near(packed))
    meta = near(meta)
    rows2, rows4, image2 = near(rows2), near(rows4), near(image2)
    direct, images = near(direct), near(images)
    res2, res135 = pl.pallas_call(
        early_kernel,
        out_shape=(many(), many(3)),
        in_specs=[VMEM] * 5,
        out_specs=(VMEM, VMEM),
        name="early",
    )(meta, rows0, rows2, image2, direct)
    res135 = pl.pallas_call(
        middle_kernel,
        out_shape=many(3),
        in_specs=[VMEM] * 5,
        out_specs=VMEM,
        input_output_aliases={4: 0},
        name="middle",
    )(meta, rows0, rows2, images, near(res135))
    res135 = pl.pallas_call(
        late_kernel,
        out_shape=many(3),
        in_specs=[VMEM] * 5,
        out_specs=VMEM,
        input_output_aliases={4: 0},
        name="late",
    )(meta, rows4, direct, images, near(res135))
    home = shift(res135, 0, 1)
    whole = jax.ShapeDtypeStruct((STEPS, 3, ri, slots), jnp.float32)
    far = pl.BlockSpec(memory_space=pl.ANY)
    evens = pl.pallas_call(
        fourth_kernel,
        out_shape=whole,
        in_specs=[VMEM] * 5,
        out_specs=far,
        scratch_shapes=[
            pltpu.VMEM((3, ri, slots), jnp.float32),
            pltpu.SemaphoreType.DMA((3,)),
        ],
        name="fourth",
    )(meta, rows4, near(image4), near(res0), near(res2))
    done = pl.pallas_call(
        final_kernel,
        out_shape=whole,
        in_specs=[VMEM, far],
        out_specs=far,
        scratch_shapes=[pltpu.SemaphoreType.DMA((3,))],
        input_output_aliases={1: 0},
        name="final",
    )(near(home), evens)
    return jnp.transpose(done, (0, 2, 1, 3))


def solution(mesh):
    return jax.shard_map(
        local,
        mesh=mesh,
        in_specs=(
            P(("row", "col"), None, None),
            P(("row", "col"), None, None),
            P(("row", "col"), None, None),
            P(),
            P(),
            P(),
            P(),
        ),
        out_specs=P(None, ("row", "col"), None, None),
        check_vma=False,
    )
```

```python
import functools

import jax
import jax.numpy as jnp
from jax import lax
from jax.experimental import pallas as pl
from jax.experimental.pallas import tpu as pltpu
from jax.sharding import PartitionSpec as P


STEPS = 6
TABLE = 8
PARTS = 4
COLS = 24
FLAGS = 32
inv_temp = 10.0
big_value = 1e30

SMEM = pl.BlockSpec(memory_space=pltpu.SMEM)
VMEM = pl.BlockSpec(memory_space=pltpu.VMEM)


def move(value, target, by_col):
    n_row, n_col = lax.axis_size("row"), lax.axis_size("col")
    perm = [
        (i * n_col + j, target(i) % n_row * n_col + (j + by_col) % n_col)
        for i in range(n_row)
        for j in range(n_col)
    ]
    return lax.ppermute(value, ("row", "col"), perm)


def shift(value, by_row, by_col):
    return move(value, lambda i: i + by_row, by_col)


def one_pair(rows, image, table, row_count, col_count):
    scores = inv_temp * lax.dot_general(
        image, rows, (((1,), (1,)), ((), ())), preferred_element_type=jnp.float32
    )
    col_ok = lax.broadcasted_iota(jnp.int32, scores.shape, 0) < col_count
    row_ok = lax.broadcasted_iota(jnp.int32, (1, scores.shape[1]), 1) < row_count
    over_col = jnp.where(col_ok, scores, -big_value)
    over_row = jnp.where(row_ok, scores, -big_value)
    row_exp = jnp.exp(over_col - jnp.max(over_col, axis=0, keepdims=True))
    col_exp = jnp.exp(over_row - jnp.max(over_row, axis=1, keepdims=True))
    row_inv = 1.0 / jnp.sum(row_exp, axis=0, keepdims=True)
    col_inv = 1.0 / jnp.sum(col_exp, axis=1, keepdims=True)
    prob = ((row_exp * row_inv) * (col_exp * col_inv)).astype(jnp.bfloat16)
    return lax.dot_general(
        table, prob, (((1,), (0,)), ((), ())), preferred_element_type=jnp.float32
    )


def panel(step, rows_ref, packed_ref, meta_ref, out_ref):
    ri = rows_ref.shape[0]
    out_ref[...] = jnp.zeros_like(out_ref)
    flags = jnp.max(meta_ref[pl.ds(FLAGS + step, 1), :].astype(jnp.float32)).astype(jnp.int32)

    slots = rows_ref.shape[1]
    half = slots // 2
    few_cols = (flags >> (2 * ri)) & 1

    def body(r, carry):
        kind = ((flags >> r) & 1) * (1 + 2 * few_cols + ((flags >> (ri + r)) & 1))

        def pair(q, k):
            found = one_pair(
                rows_ref[r, :q],
                packed_ref[:k],
                packed_ref[slots:, :k],
                meta_ref[pl.ds(step * ri + r, 1), :][:, :q],
                meta_ref[pl.ds(COLS + step, 1), :][:, :q],
            )
            if q < slots:
                rest = jnp.zeros((found.shape[0], slots - q), jnp.float32)
                found = jnp.concatenate([found, rest], axis=1)
            for c in range(3):
                out_ref[c, pl.ds(r, 1), :] = found[c : c + 1]

        for n, (q, k) in enumerate(
            ((slots, slots), (half, slots), (slots, half), (half, half))
        ):
            pl.when(kind == n + 1)(functools.partial(pair, q, k))
        return carry

    @pl.when((flags & ((1 << ri) - 1)) != 0)
    def _():
        lax.fori_loop(0, ri, body, 0)


def pack_kernel(col_desc, coords, packed, table_in, sems):
    k = col_desc.shape[1]
    part = k // PARTS
    copies = [pltpu.make_async_copy(coords, table_in, sems.at[0])] + [
        pltpu.make_async_copy(
            col_desc.at[:, n * part : (n + 1) * part],
            packed.at[:, n * part : (n + 1) * part],
            sems.at[n + 1],
        )
        for n in range(PARTS)
    ]
    for copy in copies:
        copy.start()
    copies[0].wait()
    at = lax.broadcasted_iota(jnp.int32, (TABLE, k), 0)
    x = table_in[0, 0:1].astype(jnp.float32)
    y = table_in[0, 1:2].astype(jnp.float32)
    zero = jnp.zeros((TABLE, k), jnp.float32)
    table = jnp.where(at == 0, 1.0, jnp.where(at == 1, x, jnp.where(at == 2, y, zero)))
    table = table.astype(jnp.bfloat16)
    packed[0, k:] = table
    for copy in copies[1:]:
        copy.wait()


def join_kernel(image2, image4, out):
    out[0] = image2[0]
    out[1] = image4[0]


def first_kernel(
    sizes, row_counts, col_counts, row_cluster, col_cluster, rows, packed, out, meta
):
    n_row, n_col = sizes
    ri = rows.shape[0]
    row_pos, col_pos = lax.axis_index("row"), lax.axis_index("col")
    slots = rows.shape[1]
    for step in range(STEPS):
        odd = step % 2
        block = row_pos * n_col + lax.rem(col_pos - (step - odd) + n_col, n_col)
        image = lax.rem(row_pos - step + n_row, n_row) * n_col + lax.rem(col_pos + odd, n_col)
        flags = 0
        for r in range(ri):
            same = row_cluster[block * ri + r] == col_cluster[image]
            flags += same.astype(jnp.int32) * (1 << r)
            few = row_counts[block * ri + r] <= slots // 2
            flags += few.astype(jnp.int32) * (1 << (ri + r))
            meta[pl.ds(step * ri + r, 1), :] = jnp.full(
                (1, slots), row_counts[block * ri + r], jnp.int32
            )
        meta[pl.ds(COLS + step, 1), :] = jnp.full((1, slots), col_counts[image], jnp.int32)
        few = col_counts[image] <= slots // 2
        flags += few.astype(jnp.int32) * (1 << (2 * ri))
        meta[pl.ds(FLAGS + step, 1), :] = jnp.full((1, slots), flags, jnp.int32)
    panel(0, rows, packed.at[0], meta, out)


def even_row():
    return lax.rem(lax.axis_index("row"), 2) == 0


def early_kernel(meta, rows0, rows2, image2, direct, res2, out):
    panel(2, rows2, image2.at[0], meta, res2)

    @pl.when(jnp.logical_not(even_row()))
    def _():
        panel(1, rows0, direct.at[0], meta, out.at[0])


def middle_kernel(meta, rows0, rows2, images, kept, out):
    del kept
    even = even_row()

    @pl.when(even)
    def _():
        panel(1, rows0, images.at[0], meta, out.at[0])

    panel(3, rows2, images.at[even.astype(jnp.int32)], meta, out.at[1])


def late_kernel(meta, rows4, direct, images, kept, out):
    del kept
    even = even_row()

    @pl.when(even)
    def _():
        panel(5, rows4, direct.at[0], meta, out.at[2])

    @pl.when(jnp.logical_not(even))
    def _():
        panel(5, rows4, images.at[1], meta, out.at[2])


def write_all(parts, out, sems):
    copies = [
        pltpu.make_async_copy(part, out.at[at], sems.at[n])
        for n, (part, at) in enumerate(parts)
    ]
    for copy in copies:
        copy.start()
    for copy in copies:
        copy.wait()


def fourth_kernel(meta, rows, packed, res0, res2, out, res4, sems):
    panel(4, rows, packed.at[0], meta, res4)
    write_all(((res0, 0), (res2, 2), (res4, 4)), out, sems)


def final_kernel(home, kept, out, sems):
    del kept
    write_all([(home.at[n], 2 * n + 1) for n in range(3)], out, sems)


def near(value):
    return pltpu.with_memory_space_constraint(value, pltpu.VMEM)


def local(row_desc, col_desc, col_coords, row_counts, col_counts, row_cluster, col_cluster):
    n_row, n_col = lax.axis_size("row"), lax.axis_size("col")
    ri, slots, depth = row_desc.shape
    k = slots + TABLE

    def many(*count):
        return pltpu.VMEM((*count, 3, ri, slots), jnp.float32)

    rows2 = shift(row_desc, 0, 2)
    packed = pl.pallas_call(
        pack_kernel,
        out_shape=pltpu.VMEM((1, k, depth), jnp.bfloat16),
        in_specs=[pl.BlockSpec(memory_space=pl.ANY)] * 2,
        out_specs=VMEM,
        scratch_shapes=[
            pltpu.VMEM(col_coords.shape, jnp.bfloat16),
            pltpu.SemaphoreType.DMA((PARTS + 1,)),
        ],
        name="pack",
    )(col_desc, col_coords)
    image2 = shift(packed, 2, 0)
    image4 = shift(packed, 4, 0)
    rows4 = shift(rows2, 0, 2)
    joined = pl.pallas_call(
        join_kernel,
        out_shape=pltpu.VMEM((2, k, depth), jnp.bfloat16),
        in_specs=[VMEM] * 2,
        out_specs=VMEM,
        name="join",
    )(near(image2), near(image4))
    images = move(joined, lambda i: i ^ 1, -1)
    direct = move(packed, lambda i: i + (5 if i % 2 else 1), -1)
    rows0 = near(row_desc)

    res0, meta = pl.pallas_call(
        functools.partial(first_kernel, (n_row, n_col)),
        out_shape=(many(), pltpu.VMEM((FLAGS + 8, slots), jnp.int32)),
        in_specs=[SMEM] * 4 + [VMEM] * 2,
        out_specs=(VMEM, VMEM),
        name="first",
    )(row_counts, col_counts, row_cluster, col_cluster, rows0, near(packed))
    meta = near(meta)
    rows2, rows4, image2 = near(rows2), near(rows4), near(image2)
    direct, images = near(direct), near(images)
    res2, res135 = pl.pallas_call(
        early_kernel,
        out_shape=(many(), many(3)),
        in_specs=[VMEM] * 5,
        out_specs=(VMEM, VMEM),
        name="early",
    )(meta, rows0, rows2, image2, direct)
    res135 = pl.pallas_call(
        middle_kernel,
        out_shape=many(3),
        in_specs=[VMEM] * 5,
        out_specs=VMEM,
        input_output_aliases={4: 0},
        name="middle",
    )(meta, rows0, rows2, images, near(res135))
    res135 = pl.pallas_call(
        late_kernel,
        out_shape=many(3),
        in_specs=[VMEM] * 5,
        out_specs=VMEM,
        input_output_aliases={4: 0},
        name="late",
    )(meta, rows4, direct, images, near(res135))
    home = shift(res135, 0, 1)
    whole = jax.ShapeDtypeStruct((STEPS, 3, ri, slots), jnp.float32)
    far = pl.BlockSpec(memory_space=pl.ANY)
    evens = pl.pallas_call(
        fourth_kernel,
        out_shape=whole,
        in_specs=[VMEM] * 5,
        out_specs=far,
        scratch_shapes=[
            pltpu.VMEM((3, ri, slots), jnp.float32),
            pltpu.SemaphoreType.DMA((3,)),
        ],
        name="fourth",
    )(meta, rows4, near(image4), near(res0), near(res2))
    done = pl.pallas_call(
        final_kernel,
        out_shape=whole,
        in_specs=[VMEM, far],
        out_specs=far,
        scratch_shapes=[pltpu.SemaphoreType.DMA((3,))],
        input_output_aliases={1: 0},
        name="final",
    )(near(home), evens)
    return jnp.transpose(done, (0, 2, 1, 3))


def solution(mesh):
    return jax.shard_map(
        local,
        mesh=mesh,
        in_specs=(
            P(("row", "col"), None, None),
            P(("row", "col"), None, None),
            P(("row", "col"), None, None),
            P(),
            P(),
            P(),
            P(),
        ),
        out_specs=P(None, ("row", "col"), None, None),
        check_vma=False,
    )
```

```python
import functools

import jax
import jax.numpy as jnp
from jax import lax
from jax.experimental import pallas as pl
from jax.experimental.pallas import tpu as pltpu
from jax.sharding import PartitionSpec as P


STEPS = 6
TABLE = 8
PARTS = 4
COLS = 24
FLAGS = 32
inv_temp = 10.0
log2_e = 1.4426950408889634
big_value = 1e30

SMEM = pl.BlockSpec(memory_space=pltpu.SMEM)
VMEM = pl.BlockSpec(memory_space=pltpu.VMEM)


def move(value, target, by_col):
    n_row, n_col = lax.axis_size("row"), lax.axis_size("col")
    perm = [
        (i * n_col + j, target(i) % n_row * n_col + (j + by_col) % n_col)
        for i in range(n_row)
        for j in range(n_col)
    ]
    return lax.ppermute(value, ("row", "col"), perm)


def shift(value, by_row, by_col):
    return move(value, lambda i: i + by_row, by_col)


def one_pair(rows, packed, row_count, col_count):
    k = packed.shape[0] - TABLE
    scores = (inv_temp * log2_e) * lax.dot_general(
        packed[:k], rows, (((1,), (1,)), ((), ())), preferred_element_type=jnp.float32
    )
    col_ok = lax.broadcasted_iota(jnp.int32, scores.shape, 0) < col_count
    row_ok = lax.broadcasted_iota(jnp.int32, (1, scores.shape[1]), 1) < row_count
    over_col = jnp.where(col_ok, scores, -big_value)
    over_row = jnp.where(row_ok, scores, -big_value)
    row_exp = jnp.exp2(over_col - jnp.max(over_col, axis=0, keepdims=True))
    col_exp = jnp.exp2(over_row - jnp.max(over_row, axis=1, keepdims=True))
    row_inv = 1.0 / jnp.sum(row_exp, axis=0, keepdims=True)
    col_inv = 1.0 / jnp.sum(col_exp, axis=1, keepdims=True)
    prob = ((row_exp * row_inv) * (col_exp * col_inv)).astype(jnp.bfloat16)
    return lax.dot_general(
        packed[k:], prob, (((1,), (0,)), ((), ())), preferred_element_type=jnp.float32
    )


def panel(step, rows_ref, packed_ref, meta_ref, out_ref):
    ri = rows_ref.shape[0]
    out_ref[...] = jnp.zeros_like(out_ref)
    flags = jnp.max(meta_ref[pl.ds(FLAGS + step, 1), :].astype(jnp.float32)).astype(jnp.int32)

    def body(r, carry):
        @pl.when(((flags >> r) & 1) == 1)
        def _():
            found = one_pair(
                rows_ref[r],
                packed_ref[...],
                meta_ref[pl.ds(step * ri + r, 1), :],
                meta_ref[pl.ds(COLS + step, 1), :],
            )
            for c in range(3):
                out_ref[c, pl.ds(r, 1), :] = found[c : c + 1]

        return carry

    @pl.when(flags != 0)
    def _():
        lax.fori_loop(0, ri, body, 0)


def pack_kernel(col_desc, coords, packed, table_in, sems):
    k = col_desc.shape[1]
    part = k // PARTS
    copies = [pltpu.make_async_copy(coords, table_in, sems.at[0])] + [
        pltpu.make_async_copy(
            col_desc.at[:, n * part : (n + 1) * part],
            packed.at[:, n * part : (n + 1) * part],
            sems.at[n + 1],
        )
        for n in range(PARTS)
    ]
    for copy in copies:
        copy.start()
    copies[0].wait()
    at = lax.broadcasted_iota(jnp.int32, (TABLE, k), 0)
    x = table_in[0, 0:1].astype(jnp.float32)
    y = table_in[0, 1:2].astype(jnp.float32)
    zero = jnp.zeros((TABLE, k), jnp.float32)
    table = jnp.where(at == 0, 1.0, jnp.where(at == 1, x, jnp.where(at == 2, y, zero)))
    table = table.astype(jnp.bfloat16)
    packed[0, k:] = table
    for copy in copies[1:]:
        copy.wait()


def join_kernel(image2, image4, out):
    out[0] = image2[0]
    out[1] = image4[0]


def first_kernel(
    sizes, row_counts, col_counts, row_cluster, col_cluster, rows, packed, out, meta
):
    n_row, n_col = sizes
    ri = rows.shape[0]
    row_pos, col_pos = lax.axis_index("row"), lax.axis_index("col")
    slots = rows.shape[1]
    for step in range(STEPS):
        odd = step % 2
        block = row_pos * n_col + lax.rem(col_pos - (step - odd) + n_col, n_col)
        image = lax.rem(row_pos - step + n_row, n_row) * n_col + lax.rem(col_pos + odd, n_col)
        flags = 0
        for r in range(ri):
            same = row_cluster[block * ri + r] == col_cluster[image]
            flags += same.astype(jnp.int32) * (1 << r)
            meta[pl.ds(step * ri + r, 1), :] = jnp.full(
                (1, slots), row_counts[block * ri + r], jnp.int32
            )
        meta[pl.ds(COLS + step, 1), :] = jnp.full((1, slots), col_counts[image], jnp.int32)
        meta[pl.ds(FLAGS + step, 1), :] = jnp.full((1, slots), flags, jnp.int32)
    panel(0, rows, packed.at[0], meta, out)


def even_row():
    return lax.rem(lax.axis_index("row"), 2) == 0


def early_kernel(meta, rows0, rows2, image2, direct, res2, out):
    panel(2, rows2, image2.at[0], meta, res2)

    @pl.when(jnp.logical_not(even_row()))
    def _():
        panel(1, rows0, direct.at[0], meta, out.at[0])


def middle_kernel(meta, rows0, rows2, images, kept, out):
    del kept
    even = even_row()

    @pl.when(even)
    def _():
        panel(1, rows0, images.at[0], meta, out.at[0])

    panel(3, rows2, images.at[even.astype(jnp.int32)], meta, out.at[1])


def late_kernel(meta, rows4, direct, images, kept, out):
    del kept
    even = even_row()

    @pl.when(even)
    def _():
        panel(5, rows4, direct.at[0], meta, out.at[2])

    @pl.when(jnp.logical_not(even))
    def _():
        panel(5, rows4, images.at[1], meta, out.at[2])


def write_all(parts, out, sems):
    copies = [
        pltpu.make_async_copy(part, out.at[at], sems.at[n])
        for n, (part, at) in enumerate(parts)
    ]
    for copy in copies:
        copy.start()
    for copy in copies:
        copy.wait()


def fourth_kernel(meta, rows, packed, res0, res2, out, res4, sems):
    panel(4, rows, packed.at[0], meta, res4)
    write_all(((res0, 0), (res2, 2), (res4, 4)), out, sems)


def final_kernel(home, kept, out, sems):
    del kept
    write_all([(home.at[n], 2 * n + 1) for n in range(3)], out, sems)


def near(value):
    return pltpu.with_memory_space_constraint(value, pltpu.VMEM)


def local(row_desc, col_desc, col_coords, row_counts, col_counts, row_cluster, col_cluster):
    n_row, n_col = lax.axis_size("row"), lax.axis_size("col")
    ri, slots, depth = row_desc.shape
    k = slots + TABLE

    def many(*count):
        return pltpu.VMEM((*count, 3, ri, slots), jnp.float32)

    rows2 = shift(row_desc, 0, 2)
    packed = pl.pallas_call(
        pack_kernel,
        out_shape=pltpu.VMEM((1, k, depth), jnp.bfloat16),
        in_specs=[pl.BlockSpec(memory_space=pl.ANY)] * 2,
        out_specs=VMEM,
        scratch_shapes=[
            pltpu.VMEM(col_coords.shape, jnp.bfloat16),
            pltpu.SemaphoreType.DMA((PARTS + 1,)),
        ],
        name="pack",
    )(col_desc, col_coords)
    image2 = shift(packed, 2, 0)
    image4 = shift(packed, 4, 0)
    rows4 = shift(rows2, 0, 2)
    joined = pl.pallas_call(
        join_kernel,
        out_shape=pltpu.VMEM((2, k, depth), jnp.bfloat16),
        in_specs=[VMEM] * 2,
        out_specs=VMEM,
        name="join",
    )(near(image2), near(image4))
    images = move(joined, lambda i: i ^ 1, -1)
    direct = move(packed, lambda i: i + (5 if i % 2 else 1), -1)
    rows0 = near(row_desc)

    res0, meta = pl.pallas_call(
        functools.partial(first_kernel, (n_row, n_col)),
        out_shape=(many(), pltpu.VMEM((FLAGS + 8, slots), jnp.int32)),
        in_specs=[SMEM] * 4 + [VMEM] * 2,
        out_specs=(VMEM, VMEM),
        name="first",
    )(row_counts, col_counts, row_cluster, col_cluster, rows0, near(packed))
    meta = near(meta)
    rows2, rows4, image2 = near(rows2), near(rows4), near(image2)
    direct, images = near(direct), near(images)
    res2, res135 = pl.pallas_call(
        early_kernel,
        out_shape=(many(), many(3)),
        in_specs=[VMEM] * 5,
        out_specs=(VMEM, VMEM),
        name="early",
    )(meta, rows0, rows2, image2, direct)
    res135 = pl.pallas_call(
        middle_kernel,
        out_shape=many(3),
        in_specs=[VMEM] * 5,
        out_specs=VMEM,
        input_output_aliases={4: 0},
        name="middle",
    )(meta, rows0, rows2, images, near(res135))
    res135 = pl.pallas_call(
        late_kernel,
        out_shape=many(3),
        in_specs=[VMEM] * 5,
        out_specs=VMEM,
        input_output_aliases={4: 0},
        name="late",
    )(meta, rows4, direct, images, near(res135))
    home = shift(res135, 0, 1)
    whole = jax.ShapeDtypeStruct((STEPS, 3, ri, slots), jnp.float32)
    far = pl.BlockSpec(memory_space=pl.ANY)
    evens = pl.pallas_call(
        fourth_kernel,
        out_shape=whole,
        in_specs=[VMEM] * 5,
        out_specs=far,
        scratch_shapes=[
            pltpu.VMEM((3, ri, slots), jnp.float32),
            pltpu.SemaphoreType.DMA((3,)),
        ],
        name="fourth",
    )(meta, rows4, near(image4), near(res0), near(res2))
    done = pl.pallas_call(
        final_kernel,
        out_shape=whole,
        in_specs=[VMEM, far],
        out_specs=far,
        scratch_shapes=[pltpu.SemaphoreType.DMA((3,))],
        input_output_aliases={1: 0},
        name="final",
    )(near(home), evens)
    return jnp.transpose(done, (0, 2, 1, 3))


def solution(mesh):
    return jax.shard_map(
        local,
        mesh=mesh,
        in_specs=(
            P(("row", "col"), None, None),
            P(("row", "col"), None, None),
            P(("row", "col"), None, None),
            P(),
            P(),
            P(),
            P(),
        ),
        out_specs=P(None, ("row", "col"), None, None),
        check_vma=False,
    )
```
